256 devices in a mesh: dp: 16 (over z, core), seq: 16 (over y, x).
Axes of the slice: x: 4, y: 4, z: 8, core: 2. Of those that a mesh axis runs over, the one named last changes fastest.
Arguments:
- patches: bfloat16 [12288, 6144], P(('dp', 'seq')), may hold values from -12 to 12
- destination: int32 [12288, 1], P(('dp', 'seq')), may hold values from 0 to 15; in each aligned block of 48 rows (0 to 47, 48 to 95, ...) at most 4 rows name the same one
- segments: int32 [16, 1024], P('dp'), may hold values from 0 to 7, never falling along the last dimension, each value on 1 to 256 neighbouring positions
- qkv_weight: bfloat16 [6144, 3, 4096], P(None, None, 'seq'), may hold values from -2 to 2
- cotangent: bfloat16 [16, 1024, 4096], P('dp', None, 'seq'), may hold values from -6 to 6
Outputs:
- attended: bfloat16 [16, 1024, 4096], P('dp', None, 'seq')
- dproj: bfloat16 [16, 1024, 3, 4096], P('dp', None, None, 'seq')
The draws below stay inside these ranges and needn't reach their ends.
Inputs may be any that keep to these rules, and one draw needn't show every extreme that they name: `destination`: the rows of one loader device name one pack at most 4 times. `segments`: image ids never fall along a pack; one image holds 1 to 256 slots.
All inputs are finite; a program needn't handle non-finite values.
Results may differ from the reference program's by a relative error of at most 0.009.
The reference program's roundings to bfloat16 on the way (of `packed`, `proj`, `probs_low`, `grad` and `score_grad`) count: a program that leaves them out, or rounds other values in their place, can miss the bound.
Values may be sent and summed in bfloat16 or wider, within the bound.
No kernel may reach another device: no remote copies, remote signals or barrier semaphores. Data moves between devices by JAX's collectives and lax.ppermute only.
A program may use at most 128 MiB of HBM per device.

```python
import math
import jax
import jax.numpy as jnp
import numpy as np
from jax import lax

D = 6144
HD = 128
HEADS = 32
TOK_DEV = 64
CAP = 4
LOAD_DEV = 48
ROWS = 12288
PACK_LEN = 1024
IMG_MOST = 256
IMAGES = 8
N_DP = 16
N_SEQ = 16


def draw_patches(key, part):
    first = jax.random.fold_in(key, 0)
    return jnp.clip(jax.random.normal(first, (ROWS, D), jnp.float32), -4.0, 4.0).astype(jnp.bfloat16)


def draw_qkv_weight(key, part):
    normal = jnp.clip(jax.random.normal(key, (D, 3, HEADS * HD), jnp.float32), -5.0, 5.0) / math.sqrt(D)
    return normal.astype(jnp.bfloat16)


def level_of(own_key, extent, cuts, least, largest):
    gain, own = 1.0, jax.random.fold_in(own_key, 6)
    for dim, blocks in cuts:
        draws = jnp.exp(jax.random.uniform(jax.random.fold_in(own, dim), (blocks,), jnp.float32, least / len(cuts), largest / len(cuts)))
        gain = gain * jnp.repeat(draws, extent[dim] // blocks).reshape([-1 if axis == dim else 1 for axis in range(len(extent))])
    return gain


def split_up(number_of, total, limit, skew):
    portions = [(1 << 20) // math.isqrt(rank ** skew) + 1 for rank in range(2, number_of + 1)]
    surplus, holding = total - limit - (number_of - 1), [1] * (number_of - 1)
    while surplus > 0:
        free = [i for i in range(number_of - 1) if holding[i] < limit]
        pool, budget = sum([portions[i] for i in free]), surplus
        for i in free:
            more = min(limit - holding[i], max(1, budget * portions[i] // pool), surplus)
            holding[i] = holding[i] + more
            surplus = surplus - more
    return np.array([limit] + holding)


def uneven_parts(own_key, amount, total, reach, skew):
    if amount == 2:
        one = jax.random.randint(own_key, (), max(1, total - reach), min(reach, total - 1) + 1)
        return jnp.stack([one, total - one])
    tallies = jnp.asarray(split_up(amount, total, reach, skew), jnp.int32)
    pairs = (amount - 1) // 2
    source_of, taker = tallies[1:1 + 2 * pairs:2], tallies[2:2 + 2 * pairs:2]
    room = jnp.minimum(source_of - 1, reach - taker)
    shifted = jax.random.randint(jax.random.fold_in(own_key, 1), (pairs,), 0, 1 << 20) % (room + 1)
    tallies = tallies.at[1:1 + 2 * pairs:2].set(source_of - shifted).at[2:2 + 2 * pairs:2].set(taker + shifted)
    return tallies[jax.random.permutation(jax.random.fold_in(own_key, 2), amount)]


def routed_block(rng, own, number, rows, number_of, top, reach, skew):
    ranking = jax.random.permutation(rng, number_of)
    crowded, ordinary = load_shares(number_of, rows * top, reach, skew, True), load_shares(number_of, rows * top, reach, skew, False)
    places = jnp.arange(number_of)

    def named(lengths, turn):
        used = int((lengths > 0).sum())
        fixed = max(1, used // 4)
        moved = fixed + (places - fixed + turn * (used - fixed)) % max(1, number_of - fixed)
        return jnp.zeros((number_of,), jnp.int32).at[ranking[jnp.where(places < fixed, places, moved)]].set(jnp.asarray(lengths, jnp.int32))

    lengths = jnp.where(number % 4 == 0, named(crowded, number // 4), named(ordinary, number - number // 4 - 1))
    mixed = jax.random.permutation(jax.random.fold_in(own, 3), number_of)
    donor, receiver = mixed[0:number_of // 2 * 2:2], mixed[1:number_of // 2 * 2:2]
    margin = jnp.minimum(lengths[donor] - 1, reach - lengths[receiver]) // 2
    margin = jnp.where((donor == ranking[0]) | (receiver == ranking[0]) | (lengths[receiver] == 0), 0, jnp.maximum(margin, 0))
    moved = jax.random.randint(jax.random.fold_in(own, 4), (number_of // 2,), 0, 1 << 20) % (margin + 1)
    lengths = lengths.at[donor].add(-moved).at[receiver].add(moved)
    items = jnp.searchsorted(jnp.cumsum(lengths), jnp.arange(rows * top), side="right").astype(jnp.int32)
    table = items.reshape(top, rows).T
    table = table[jax.random.permutation(jax.random.fold_in(own, 1), rows)]
    turn = jax.random.randint(jax.random.fold_in(own, 2), (rows, 1), 0, top)
    return jnp.take_along_axis(table, (jnp.arange(top)[None, :] + turn) % top, axis=1)


def load_shares(amount, total, most, slope, full):
    weights = [(1 << 20) // math.isqrt(rank ** slope) + 1 for rank in range(1, amount + 1)]
    largest = most if full else min(most, max(-(-total // amount), total * weights[0] // sum(weights)))
    least = 1 if total - largest >= amount - 1 else 0
    given, spare = [largest] + [least] * (amount - 1), total - largest - least * (amount - 1)
    while spare > 0:
        free = [i for i in range(1, amount) if given[i] < largest] or [i for i in range(1, amount) if given[i] < most]
        whole, left = sum([weights[i] for i in free]), spare
        for i in free:
            extra = min(most - given[i], max(1, left * weights[i] // whole), spare)
            given[i] = given[i] + extra
            spare = spare - extra
    return np.array(given)


def bell_draw(own_key, shape, width, bound, shards=(), held_as=jnp.bfloat16):
    values = jax.random.normal(own_key, shape, jnp.float32) * width
    if len(shards) > 0:
        values = level_of(own_key, shape, shards, -0.22, 0.18) * values
    return jnp.clip(values, min=-bound, max=bound).astype(held_as)


def setup_inputs(seed: int = 0) -> dict:
    splits = jax.random.split(jax.random.key(seed), 6)
    patches = draw_patches(jax.random.fold_in(splits[5], 71), 0)
    destination_keys = jax.random.split(jax.random.fold_in(splits[1], 1), ROWS // LOAD_DEV)
    destination_turns = jax.random.permutation(jax.random.fold_in(splits[1], 3), ROWS // LOAD_DEV)
    destination = jax.vmap(lambda own, number: routed_block(jax.random.fold_in(splits[1], 2), own, number, LOAD_DEV, N_DP, 1, CAP, 2))(destination_keys, destination_turns).reshape((ROWS, 1))
    segments = jax.vmap(lambda own: jnp.searchsorted(jnp.cumsum(uneven_parts(own, IMAGES, PACK_LEN, IMG_MOST, 2)), jnp.arange(PACK_LEN), side="right"))(jax.random.split(splits[2], N_DP)).reshape((N_DP, PACK_LEN)).astype(jnp.int32)
    qkv_weight = draw_qkv_weight(jax.random.fold_in(splits[5], 71), 0)
    cotangent = bell_draw(splits[4], (N_DP, PACK_LEN, HEADS * HD), 1.0, 6.0, ((0, 16), (2, 16)))
    return {"patches": patches, "destination": destination, "segments": segments, "qkv_weight": qkv_weight, "cotangent": cotangent}


def place_rows(patches, destination):
    target = destination[:, 0].astype(jnp.int32)
    loader = jnp.arange(ROWS, dtype=jnp.int32) // LOAD_DEV
    loader_dp = loader // N_SEQ
    loader_seq = loader % N_SEQ
    onehot = (target[:, None] == jnp.arange(N_DP, dtype=jnp.int32)[None, :]).astype(jnp.int32)
    blocks = onehot.reshape(N_DP * N_SEQ, LOAD_DEV, N_DP)
    before = (jnp.cumsum(blocks, axis=1) - blocks).reshape(ROWS, N_DP)
    rank = jnp.sum(before * onehot, axis=1).astype(jnp.int32)
    position = target * PACK_LEN + loader_seq * TOK_DEV + loader_dp * CAP + rank
    packed = jnp.zeros((N_DP * PACK_LEN, D), jnp.bfloat16).at[position].set(patches)
    live = jnp.zeros((N_DP * PACK_LEN,), jnp.float32).at[position].set(1.0)
    return packed.reshape(N_DP, PACK_LEN, D), live.reshape(N_DP, PACK_LEN)


def head_pass(query, key_mat, value, seg, live, grad):
    scale = HD ** -0.5
    scores = jnp.dot(query, key_mat.T, preferred_element_type=jnp.float32) * scale
    allowed = (seg[:, None] == seg[None, :]) & (live[None, :] > 0)
    scores = jnp.where(allowed, scores, -1.0e9)
    top = jnp.max(scores, axis=1, keepdims=True)
    expo = jnp.exp(scores - top)
    probs = expo / jnp.sum(expo, axis=1, keepdims=True)
    probs_low = probs.astype(jnp.bfloat16)
    context = jnp.dot(probs_low, value, preferred_element_type=jnp.float32)
    result = (context * live[:, None]).astype(jnp.bfloat16)
    row_delta = jnp.sum(grad.astype(jnp.float32) * context, axis=1)
    prob_grad = jnp.dot(grad, value.T, preferred_element_type=jnp.float32)
    score_grad = (probs * (prob_grad - row_delta[:, None])).astype(jnp.bfloat16)
    query_grad = (jnp.dot(score_grad, key_mat, preferred_element_type=jnp.float32) * scale).astype(jnp.bfloat16)
    key_grad = (jnp.dot(score_grad.T, query, preferred_element_type=jnp.float32) * scale).astype(jnp.bfloat16)
    value_grad = jnp.dot(probs_low.T, grad, preferred_element_type=jnp.float32).astype(jnp.bfloat16)
    return result, query_grad, key_grad, value_grad


def reference(patches, destination, segments, qkv_weight, cotangent):
    packed, live = place_rows(patches, destination)
    flat_weight = qkv_weight.reshape(D, 3 * HEADS * HD)

    def pack_pass(inputs):
        rows, live_row, seg, cot = inputs
        proj = jnp.dot(rows, flat_weight, preferred_element_type=jnp.float32).astype(jnp.bfloat16)
        per_head = jnp.transpose(proj.reshape(PACK_LEN, 3, HEADS, HD), (2, 1, 0, 3))
        grad = (cot * live_row.astype(jnp.bfloat16)[:, None]).reshape(PACK_LEN, HEADS, HD)
        grad = jnp.transpose(grad, (1, 0, 2))

        def one_head(items):
            parts, head_grad = items
            return head_pass(parts[0], parts[1], parts[2], seg, live_row, head_grad)

        result, query_grad, key_grad, value_grad = lax.map(one_head, (per_head, grad))
        result = jnp.transpose(result, (1, 0, 2)).reshape(PACK_LEN, HEADS * HD)
        stacked = jnp.stack([query_grad, key_grad, value_grad], axis=0)
        stacked = jnp.transpose(stacked, (2, 0, 1, 3)).reshape(PACK_LEN, 3, HEADS * HD)
        return result, stacked

    attended, dproj = lax.map(pack_pass, (packed, live, segments, cotangent))
    return attended, dproj
```

```python
import jax
import jax.numpy as jnp
from jax import lax
from jax.experimental import pallas as pl
from jax.experimental.pallas import tpu as pltpu
from jax.sharding import PartitionSpec as P

HD = 128
SIDE = 4
CAP = 4
FILL = -1000000000.0
EMPTY = 1.0e15
EDGE = 128

ROUNDS = (
    (((1, 0), (1, 0)), ((3, 0), (3, 0)), ((0, 1), (0, 1)), ((0, 3), (0, 3))),
    (((1, 1), (1, 0)), ((3, 1), (0, 1)), ((3, 3), (3, 0)), ((1, 3), (0, 3))),
    (((2, 1), (1, 0)), ((2, 3), (3, 0)), ((3, 2), (0, 1)), ((1, 2), (0, 3))),
    (((2, 0), (1, 0)), ((0, 2), (0, 1)), ((2, 2), (3, 0))),
)


def mark_rows(patches, destination):
    rows, width = patches.shape

    def body(x_ref, t_ref, o_ref):
        o_ref[:, :width] = x_ref[...]
        target = t_ref[...]
        owner = lax.broadcasted_iota(jnp.int32, (rows, EDGE), 1)
        onehot = (target == owner).astype(jnp.float32)
        r = lax.broadcasted_iota(jnp.int32, (rows, rows), 0)
        c = lax.broadcasted_iota(jnp.int32, (rows, rows), 1)
        lower = (c < r).astype(jnp.bfloat16)
        before = jnp.dot(lower, onehot.astype(jnp.bfloat16), preferred_element_type=jnp.float32)
        rank = jnp.sum(before * onehot, axis=1, keepdims=True)
        slot = target.astype(jnp.float32) * CAP + rank
        o_ref[:, width:] = jnp.broadcast_to(slot, (rows, EDGE)).astype(jnp.bfloat16)

    return pl.pallas_call(
        body,
        out_shape=jax.ShapeDtypeStruct((rows, width + EDGE), jnp.bfloat16),
        name="mark_rows",
    )(patches, destination)


def project(blocks, weight, owners):
    count = len(blocks)
    rows = blocks[0].shape[0]
    width, cols = weight.shape
    step = 1024
    steps = width // step
    slots = owners * CAP * count

    def body(*refs):
        x_refs = refs[:count]
        w_ref, o_ref, all_x, acc = refs[count:]
        k = pl.program_id(0)

        @pl.when(k == 0)
        def _():
            for i in range(count):
                for j in range(steps):
                    all_x[j, i * rows : (i + 1) * rows, :] = x_refs[i][:, j * step : (j + 1) * step]

        part = jnp.dot(all_x[k], w_ref[...], preferred_element_type=jnp.float32)

        @pl.when(k == 0)
        def _():
            acc[...] = part

        @pl.when(k > 0)
        def _():
            acc[...] += part

        @pl.when(k == steps - 1)
        def _():
            done = acc[...].astype(jnp.bfloat16)
            picks = []
            for i in range(count):
                code = x_refs[i][:, width:].astype(jnp.float32)[:, :1].astype(jnp.int32)
                slot = (code // CAP) * (CAP * count) + i * CAP + code % CAP
                place = lax.broadcasted_iota(jnp.int32, (rows, slots), 1)
                picks.append((slot == place).astype(jnp.bfloat16))
            pick = jnp.concatenate(picks, axis=0)
            down = (((0,), (0,)), ((), ()))
            placed = lax.dot_general(pick, done, down, preferred_element_type=jnp.float32)
            ones = jnp.ones((count * rows, EDGE), jnp.bfloat16)
            filled = lax.dot_general(pick, ones, down, preferred_element_type=jnp.float32)
            placed = jnp.where(filled[:, :1] > 0, placed, EMPTY)
            o_ref[...] = placed.astype(jnp.bfloat16).reshape(owners, CAP * count, cols)

    full = pl.BlockSpec((rows, width + EDGE), lambda k: (0, 0))
    return pl.pallas_call(
        body,
        grid=(steps,),
        in_specs=[full] * count + [pl.BlockSpec((step, cols), lambda k: (k, 0))],
        out_specs=pl.BlockSpec((owners, CAP * count, cols), lambda k: (0, 0, 0)),
        out_shape=jax.ShapeDtypeStruct((owners, CAP * count, cols), jnp.bfloat16),
        scratch_shapes=[
            pltpu.VMEM((steps, count * rows, step), jnp.bfloat16),
            pltpu.VMEM((count * rows, cols), jnp.float32),
        ],
        compiler_params=pltpu.CompilerParams(vmem_limit_bytes=40 << 20),
        cost_estimate=pl.CostEstimate(
            flops=2 * count * rows * width * cols,
            transcendentals=0,
            bytes_accessed=2 * width * cols + 2 * count * rows * width,
        ),
        name="project",
    )(*blocks, weight)


def attention(parts, where_to, segments, cotangent):
    owners, per_owner, cols = parts[0].shape
    sources = per_owner // CAP
    pack_len = cotangent.shape[0]
    third = cols // 3
    heads = third // HD
    chunk = owners * per_owner
    span = owners * CAP
    block = 256
    blocks = pack_len // block
    scale = HD ** (-0.5)
    nt = (((1,), (1,)), ((), ()))
    tn = (((0,), (0,)), ((), ()))
    f32 = jnp.float32

    def body(*refs):
        part_refs = refs[: len(parts)]
        to_ref, segk_ref, segq_ref, cot_ref, out_ref, grad_ref, qkv, keep, codes, dk, dv, low = refs[len(parts) :]
        new = lax.broadcasted_iota(jnp.int32, (chunk, chunk), 0)
        old = lax.broadcasted_iota(jnp.int32, (chunk, chunk), 1)
        source, rest = new // span, new % span
        move = ((rest // CAP) * per_owner + source * CAP + rest % CAP == old).astype(jnp.bfloat16)
        for c in range(len(parts)):
            flat = part_refs[c][...].reshape(chunk, cols)
            moved = jnp.dot(move, flat, preferred_element_type=f32).astype(jnp.bfloat16)
            for i in range(sources):
                at = pl.multiple_of(to_ref[c * sources + i] * span, span)
                qkv[pl.ds(at, span), :] = moved[i * span : (i + 1) * span, :]
        for b in range(blocks):
            at = b * block
            lead = qkv[at : at + block, :HD].astype(f32)
            live = (lead < 0.5 * EMPTY).astype(f32)
            keep[at : at + block, :] = live
            held = qkv[at : at + block, :]
            qkv[at : at + block, :] = jnp.where(live[:, :1] > 0, held, jnp.zeros_like(held))
            live_row = (lead.T[:1, :] < 0.5 * EMPTY)
            seg = segk_ref[:, at : at + block]
            codes[:, at : at + block] = jnp.where(live_row, seg, -1)

        def clear():
            dk[...] = jnp.zeros_like(dk)
            dv[...] = jnp.zeros_like(dv)
            low[...] = jnp.zeros_like(low)

        def work(at, start, size):
            rows = pl.ds(at, block)
            win = pl.ds(start, size)
            live = keep[rows, :]
            allowed = segq_ref[rows, :] == codes[:, win]
            for h in range(heads):
                lanes = slice(h * HD, (h + 1) * HD)
                q = qkv[rows, h * HD : (h + 1) * HD]
                k = qkv[win, third + h * HD : third + (h + 1) * HD]
                v = qkv[win, 2 * third + h * HD : 2 * third + (h + 1) * HD]
                s = lax.dot_general(q, k, nt, preferred_element_type=f32) * scale
                s = jnp.where(allowed, s, FILL)
                top = jnp.max(s, axis=1, keepdims=True)
                e = jnp.exp(s - top)
                p = e * (1.0 / jnp.sum(e, axis=1, keepdims=True))
                p_low = p.astype(jnp.bfloat16)
                context = jnp.dot(p_low, v, preferred_element_type=f32)
                out_ref[rows, lanes] = (context * live).astype(jnp.bfloat16)
                g32 = cot_ref[rows, lanes].astype(f32) * live
                g = g32.astype(jnp.bfloat16)
                delta = jnp.sum(g32 * context, axis=1, keepdims=True)
                dp = lax.dot_general(g, v, nt, preferred_element_type=f32)
                ds = (p * (dp - delta)).astype(jnp.bfloat16)
                dq = jnp.dot(ds, k, preferred_element_type=f32) * scale
                grad_ref[rows, lanes] = dq.astype(jnp.bfloat16)
                dk[win, lanes] += lax.dot_general(ds, q, tn, preferred_element_type=f32)
                dv[win, lanes] += lax.dot_general(p_low, g, tn, preferred_element_type=f32)
                low[...] = jnp.minimum(low[...], jnp.min(jnp.where(live > 0, top, 0.0), axis=0, keepdims=True))

        clear()
        for b in range(blocks):
            first, last = max(b - 1, 0), min(b + 2, blocks)
            work(b * block, first * block, (last - first) * block)

        @pl.when(jnp.min(low[...]) < 0.5 * FILL)
        def _():
            clear()

            def again(b, carry):
                work(pl.multiple_of(b * block, block), 0, pack_len)
                return carry

            lax.fori_loop(0, blocks, again, 0)

        grad_ref[:, third : 2 * third] = (dk[...] * scale).astype(jnp.bfloat16)
        grad_ref[:, 2 * third :] = dv[...].astype(jnp.bfloat16)

    vmem = pl.BlockSpec(memory_space=pltpu.VMEM)
    return pl.pallas_call(
        body,
        in_specs=[vmem] * len(parts) + [pl.BlockSpec(memory_space=pltpu.SMEM)] + [vmem] * 3,
        out_specs=[vmem, vmem],
        out_shape=[
            jax.ShapeDtypeStruct((pack_len, third), jnp.bfloat16),
            jax.ShapeDtypeStruct((pack_len, cols), jnp.bfloat16),
        ],
        scratch_shapes=[
            pltpu.VMEM((pack_len, cols), jnp.bfloat16),
            pltpu.VMEM((pack_len, HD), f32),
            pltpu.VMEM((1, pack_len), jnp.int32),
            pltpu.VMEM((pack_len, third), f32),
            pltpu.VMEM((pack_len, third), f32),
            pltpu.VMEM((8, HD), f32),
        ],
        compiler_params=pltpu.CompilerParams(vmem_limit_bytes=50 << 20),
        cost_estimate=pl.CostEstimate(
            flops=12 * pack_len * pack_len * third, transcendentals=pack_len * pack_len * heads, bytes_accessed=1 << 23
        ),
        name="attention",
    )(*parts, where_to, segments, segments.reshape(pack_len, 1), cotangent)


def receive(block, link):
    pairs = [
        (((y + link[1]) % SIDE) * SIDE + (x + link[0]) % SIDE, y * SIDE + x)
        for y in range(SIDE)
        for x in range(SIDE)
    ]
    return lax.ppermute(block, "seq", pairs)


def per_device(patches, destination, segments, qkv_weight, cotangent):
    owners = lax.axis_size("dp")
    width = patches.shape[1]
    cols = 3 * qkv_weight.shape[2]
    pack_len = segments.shape[1]
    weight = qkv_weight.reshape(width, cols)

    held = {(0, 0): mark_rows(patches, destination)}
    groups = []
    for turn in ROUNDS:
        for (dx, dy), (lx, ly) in turn:
            held[dx, dy] = receive(held[(dx - lx) % SIDE, (dy - ly) % SIDE], (lx, ly))
        groups.append([offset for offset, _ in turn])
    groups[-1].append((0, 0))

    here = lax.axis_index("seq")
    hx, hy = here % SIDE, here // SIDE
    where_to = jnp.stack([((hy + dy) % SIDE) * SIDE + (hx + dx) % SIDE for group in groups for dx, dy in group])

    parts = []
    for group in groups:
        placed = project([held[offset] for offset in group], weight, owners)
        parts.append(lax.all_to_all(placed, "dp", split_axis=0, concat_axis=0, tiled=True))
    attended, grads = attention(parts, where_to, segments, cotangent[0])
    return attended[None], grads.reshape(1, pack_len, 3, cols // 3)


def solution(mesh):
    in_specs = (
        P(("dp", "seq"), None),
        P(("dp", "seq"), None),
        P("dp", None),
        P(None, None, "seq"),
        P("dp", None, "seq"),
    )
    out_specs = (P("dp", None, "seq"), P("dp", None, None, "seq"))
    return jax.shard_map(per_device, mesh=mesh, in_specs=in_specs, out_specs=out_specs, check_vma=False)
```

```python
import jax
import jax.numpy as jnp
from jax import lax
from jax.experimental import pallas as pl
from jax.experimental.pallas import tpu as pltpu
from jax.sharding import PartitionSpec as P

HD = 128
SIDE = 4
CAP = 4
FILL = -1000000000.0
EMPTY = 1.0e15
EDGE = 128
STEPS = 2

ROUNDS = (
    (((1, 0), (1, 0)), ((3, 0), (3, 0)), ((0, 1), (0, 1)), ((0, 3), (0, 3))),
    (((1, 1), (1, 0)), ((3, 1), (0, 1)), ((3, 3), (3, 0)), ((1, 3), (0, 3))),
    (((2, 1), (1, 0)), ((2, 3), (3, 0)), ((3, 2), (0, 1)), ((1, 2), (0, 3))),
    (((2, 0), (1, 0)), ((0, 2), (0, 1)), ((2, 2), (3, 0))),
)


def mark_rows(patches, destination):
    rows, width = patches.shape

    def body(x_ref, t_ref, o_ref):
        o_ref[:, :width] = x_ref[...]
        owner = lax.broadcasted_iota(jnp.int32, (EDGE, rows), 0)
        onehot = (t_ref[...] == owner).astype(jnp.bfloat16)
        r = lax.broadcasted_iota(jnp.int32, (rows, rows), 0)
        c = lax.broadcasted_iota(jnp.int32, (rows, rows), 1)
        earlier = (r < c).astype(jnp.bfloat16)
        before = jnp.dot(onehot, earlier, preferred_element_type=jnp.float32)
        rank = (before * onehot.astype(jnp.float32)).astype(jnp.bfloat16)
        number = (lax.broadcasted_iota(jnp.int32, (EDGE, EDGE), 0) * CAP).astype(jnp.float32).astype(jnp.bfloat16)
        tn = (((0,), (0,)), ((), ()))
        slot = lax.dot_general(onehot, number, tn, preferred_element_type=jnp.float32)
        slot += lax.dot_general(rank, jnp.ones((EDGE, EDGE), jnp.bfloat16), tn, preferred_element_type=jnp.float32)
        o_ref[:, width:] = slot.astype(jnp.bfloat16)

    return pl.pallas_call(
        body,
        out_shape=jax.ShapeDtypeStruct((rows, width + EDGE), jnp.bfloat16),
        name="mark_rows",
    )(patches, destination.reshape(1, rows))


def project(blocks, weight, owners):
    count = len(blocks)
    rows = blocks[0].shape[0]
    kinds, width, third = weight.shape
    cols = kinds * third
    each = CAP * count
    slots = owners * each
    step = width // STEPS

    def body(*refs):
        x_refs = refs[:count]
        w_ref, o_ref, all_x, acc = refs[count:]
        part = pl.program_id(0)

        @pl.when(part == 0)
        def _():
            for i in range(count):
                for n in range(STEPS):
                    all_x[n, i * rows : (i + 1) * rows, :] = x_refs[i][:, n * step : (n + 1) * step]
            acc[...] = jnp.zeros_like(acc)

        for j in range(kinds):
            lanes = slice(j * third, (j + 1) * third)
            acc[:, lanes] += jnp.dot(all_x[part], w_ref[j], preferred_element_type=jnp.float32)

        @pl.when(part == STEPS - 1)
        def _():
            nt = (((1,), (1,)), ((), ()))
            lead = (lax.broadcasted_iota(jnp.int32, (8, EDGE), 1) == 0).astype(jnp.bfloat16)
            edge = jnp.concatenate([x_refs[i][:, width:] for i in range(count)], axis=0)
            code = lax.dot_general(lead, edge, nt, preferred_element_type=jnp.float32)[:1].astype(jnp.int32)
            row = lax.broadcasted_iota(jnp.int32, (1, count * rows), 1)
            slot = (code // CAP) * each + (row // rows) * CAP + code % CAP
            pick = (lax.broadcasted_iota(jnp.int32, (slots, count * rows), 0) == slot).astype(jnp.bfloat16)
            ones = jnp.ones((count * rows, EDGE), jnp.bfloat16)
            filled = jnp.dot(pick, ones, preferred_element_type=jnp.float32)[:, :1] > 0
            for j in range(kinds):
                lanes = slice(j * third, (j + 1) * third)
                placed = jnp.dot(pick, acc[:, lanes].astype(jnp.bfloat16), preferred_element_type=jnp.float32)
                placed = jnp.where(filled, placed, EMPTY).astype(jnp.bfloat16)
                o_ref[:, :, lanes] = placed.reshape(owners, each, third)

    full = pl.BlockSpec((rows, width + EDGE), lambda part: (0, 0))
    return pl.pallas_call(
        body,
        grid=(STEPS,),
        in_specs=[full] * count + [pl.BlockSpec((kinds, step, third), lambda part: (0, part, 0))],
        out_specs=pl.BlockSpec((owners, each, cols), lambda part: (0, 0, 0)),
        out_shape=jax.ShapeDtypeStruct((owners, each, cols), jnp.bfloat16),
        scratch_shapes=[
            pltpu.VMEM((STEPS, count * rows, step), jnp.bfloat16),
            pltpu.VMEM((count * rows, cols), jnp.float32),
        ],
        compiler_params=pltpu.CompilerParams(vmem_limit_bytes=40 << 20),
        cost_estimate=pl.CostEstimate(
            flops=2 * count * rows * width * cols,
            transcendentals=0,
            bytes_accessed=2 * width * cols + 2 * count * rows * width,
        ),
        name="project",
    )(*blocks, pltpu.with_memory_space_constraint(weight, pltpu.HBM))


def attention(parts, where_to, segments, cotangent):
    owners, _, cols = parts[0].shape
    sources = SIDE
    per_owner = sources * CAP
    pack_len = cotangent.shape[0]
    third = cols // 3
    heads = third // HD
    chunk = owners * per_owner
    span = owners * CAP
    block = 256
    blocks = pack_len // block
    scale = HD ** (-0.5)
    nt = (((1,), (1,)), ((), ()))
    tn = (((0,), (0,)), ((), ()))
    f32 = jnp.float32

    def body(*refs):
        part_refs = refs[: len(parts)]
        to_ref, segk_ref, segq_ref, cot_ref, out_ref, grad_ref, qkv, keep, codes, dk, dv, low = refs[len(parts) :]
        new = lax.broadcasted_iota(jnp.int32, (chunk, chunk), 0)
        old = lax.broadcasted_iota(jnp.int32, (chunk, chunk), 1)
        source, rest = new // span, new % span
        move = ((rest // CAP) * per_owner + source * CAP + rest % CAP == old).astype(jnp.bfloat16)
        pieces = [(ref, n) for ref in part_refs for n in range(0, ref.shape[1], per_owner)]
        for c, (ref, n) in enumerate(pieces):
            flat = ref[:, n : n + per_owner, :].reshape(chunk, cols)
            moved = jnp.dot(move, flat, preferred_element_type=f32).astype(jnp.bfloat16)
            for i in range(sources):
                at = pl.multiple_of(to_ref[c * sources + i] * span, span)
                qkv[pl.ds(at, span), :] = moved[i * span : (i + 1) * span, :]
        for b in range(blocks):
            at = b * block
            lead = qkv[at : at + block, :HD].astype(f32)
            live = (lead < 0.5 * EMPTY).astype(f32)
            keep[at : at + block, :] = live
            held = qkv[at : at + block, :]
            qkv[at : at + block, :] = jnp.where(live[:, :1] > 0, held, jnp.zeros_like(held))
            live_row = (lead.T[:1, :] < 0.5 * EMPTY)
            seg = segk_ref[:, at : at + block]
            codes[:, at : at + block] = jnp.where(live_row, seg, -1)

        def clear():
            dk[...] = jnp.zeros_like(dk)
            dv[...] = jnp.zeros_like(dv)
            low[...] = jnp.zeros_like(low)

        def work(at, start, size):
            rows = pl.ds(at, block)
            win = pl.ds(start, size)
            live = keep[rows, :]
            allowed = segq_ref[rows, :] == codes[:, win]
            for h in range(heads):
                lanes = slice(h * HD, (h + 1) * HD)
                q = qkv[rows, h * HD : (h + 1) * HD]
                k = qkv[win, third + h * HD : third + (h + 1) * HD]
                v = qkv[win, 2 * third + h * HD : 2 * third + (h + 1) * HD]
                s = lax.dot_general(q, k, nt, preferred_element_type=f32) * scale
                s = jnp.where(allowed, s, FILL)
                top = jnp.max(s, axis=1, keepdims=True)
                e = jnp.exp(s - top)
                p = e * (1.0 / jnp.sum(e, axis=1, keepdims=True))
                p_low = p.astype(jnp.bfloat16)
                context = jnp.dot(p_low, v, preferred_element_type=f32)
                out_ref[rows, lanes] = (context * live).astype(jnp.bfloat16)
                g32 = cot_ref[rows, lanes].astype(f32) * live
                g = g32.astype(jnp.bfloat16)
                delta = jnp.sum(g32 * context, axis=1, keepdims=True)
                dp = lax.dot_general(g, v, nt, preferred_element_type=f32)
                ds = (p * (dp - delta)).astype(jnp.bfloat16)
                dq = jnp.dot(ds, k, preferred_element_type=f32) * scale
                grad_ref[0, rows, lanes] = dq.astype(jnp.bfloat16)
                dk[win, lanes] += lax.dot_general(ds, q, tn, preferred_element_type=f32)
                dv[win, lanes] += lax.dot_general(p_low, g, tn, preferred_element_type=f32)
                low[...] = jnp.minimum(low[...], jnp.min(jnp.where(live > 0, top, 0.0), axis=0, keepdims=True))

        clear()
        for b in range(blocks):
            first, last = max(b - 1, 0), min(b + 2, blocks)
            work(b * block, first * block, (last - first) * block)

        @pl.when(jnp.min(low[...]) < 0.5 * FILL)
        def _():
            clear()

            def again(b, carry):
                work(pl.multiple_of(b * block, block), 0, pack_len)
                return carry

            lax.fori_loop(0, blocks, again, 0)

        grad_ref[1] = (dk[...] * scale).astype(jnp.bfloat16)
        grad_ref[2] = dv[...].astype(jnp.bfloat16)

    vmem = pl.BlockSpec(memory_space=pltpu.VMEM)
    return pl.pallas_call(
        body,
        in_specs=[vmem] * len(parts) + [pl.BlockSpec(memory_space=pltpu.SMEM)] + [vmem] * 3,
        out_specs=[vmem, vmem],
        out_shape=[
            jax.ShapeDtypeStruct((pack_len, third), jnp.bfloat16),
            jax.ShapeDtypeStruct((3, pack_len, third), jnp.bfloat16),
        ],
        scratch_shapes=[
            pltpu.VMEM((pack_len, cols), jnp.bfloat16),
            pltpu.VMEM((pack_len, HD), f32),
            pltpu.VMEM((1, pack_len), jnp.int32),
            pltpu.VMEM((pack_len, third), f32),
            pltpu.VMEM((pack_len, third), f32),
            pltpu.VMEM((8, HD), f32),
        ],
        compiler_params=pltpu.CompilerParams(vmem_limit_bytes=50 << 20),
        cost_estimate=pl.CostEstimate(
            flops=12 * pack_len * pack_len * third, transcendentals=pack_len * pack_len * heads, bytes_accessed=1 << 23
        ),
        name="attention",
    )(*parts, where_to, segments, segments.reshape(pack_len, 1), cotangent)


def receive(block, link):
    pairs = [
        (((y + link[1]) % SIDE) * SIDE + (x + link[0]) % SIDE, y * SIDE + x)
        for y in range(SIDE)
        for x in range(SIDE)
    ]
    return lax.ppermute(block, "seq", pairs)


def per_device(patches, destination, segments, qkv_weight, cotangent):
    owners = lax.axis_size("dp")
    weight = jnp.transpose(qkv_weight, (1, 0, 2))

    held = {(0, 0): mark_rows(patches, destination)}
    for turn in ROUNDS:
        for (dx, dy), (lx, ly) in turn:
            held[dx, dy] = receive(held[(dx - lx) % SIDE, (dy - ly) % SIDE], (lx, ly))
    order = [offset for turn in ROUNDS for offset, _ in turn] + [(0, 0)]
    arrived = [order[:4], order[4:8], order[8:12], order[12:]]
    parts = []
    for offsets in arrived:
        placed = project([held[offset] for offset in offsets], weight, owners)
        parts.append(lax.all_to_all(placed, "dp", split_axis=0, concat_axis=0, tiled=True))

    here = lax.axis_index("seq")
    hx, hy = here % SIDE, here // SIDE
    where_to = jnp.stack([((hy + dy) % SIDE) * SIDE + (hx + dx) % SIDE for turn in arrived for dx, dy in turn])

    attended, grads = attention(parts, where_to, segments, cotangent[0])
    return attended[None], jnp.transpose(grads, (1, 0, 2))[None]


def solution(mesh):
    in_specs = (
        P(("dp", "seq"), None),
        P(("dp", "seq"), None),
        P("dp", None),
        P(None, None, "seq"),
        P("dp", None, "seq"),
    )
    out_specs = (P("dp", None, "seq"), P("dp", None, None, "seq"))
    return jax.shard_map(per_device, mesh=mesh, in_specs=in_specs, out_specs=out_specs, check_vma=False)
```

```python
import jax
import jax.numpy as jnp
from jax import lax
from jax.experimental import pallas as pl
from jax.experimental.pallas import tpu as pltpu
from jax.sharding import PartitionSpec as P

HD = 128
SIDE = 4
CAP = 4
FILL = -1000000000.0
EMPTY = 1.0e15
EDGE = 128
STEPS = 2

ROUNDS = (
    (((1, 0), (1, 0)), ((3, 0), (3, 0)), ((0, 1), (0, 1)), ((0, 3), (0, 3))),
    (((1, 1), (1, 0)), ((3, 1), (0, 1)), ((3, 3), (3, 0)), ((1, 3), (0, 3))),
    (((2, 1), (1, 0)), ((2, 3), (3, 0)), ((3, 2), (0, 1)), ((1, 2), (0, 3))),
    (((2, 0), (1, 0)), ((0, 2), (0, 1)), ((2, 2), (3, 0))),
)


def mark_rows(patches, destination):
    rows, width = patches.shape

    def body(x_ref, t_ref, o_ref):
        o_ref[:, :width] = x_ref[...]
        owner = lax.broadcasted_iota(jnp.int32, (EDGE, rows), 0)
        onehot = (t_ref[...] == owner).astype(jnp.bfloat16)
        r = lax.broadcasted_iota(jnp.int32, (rows, rows), 0)
        c = lax.broadcasted_iota(jnp.int32, (rows, rows), 1)
        earlier = (r < c).astype(jnp.bfloat16)
        before = jnp.dot(onehot, earlier, preferred_element_type=jnp.float32)
        rank = (before * onehot.astype(jnp.float32)).astype(jnp.bfloat16)
        number = (lax.broadcasted_iota(jnp.int32, (EDGE, EDGE), 0) * CAP).astype(jnp.float32).astype(jnp.bfloat16)
        tn = (((0,), (0,)), ((), ()))
        slot = lax.dot_general(onehot, number, tn, preferred_element_type=jnp.float32)
        slot += lax.dot_general(rank, jnp.ones((EDGE, EDGE), jnp.bfloat16), tn, preferred_element_type=jnp.float32)
        o_ref[:, width:] = slot.astype(jnp.bfloat16)

    return pl.pallas_call(
        body,
        out_shape=jax.ShapeDtypeStruct((rows, width + EDGE), jnp.bfloat16),
        name="mark_rows",
    )(patches, destination.reshape(1, rows))


def project(blocks, weight, owners):
    count = len(blocks)
    rows = blocks[0].shape[0]
    kinds, width, third = weight.shape
    cols = kinds * third
    each = CAP * count
    slots = owners * each
    step = width // STEPS

    def body(*refs):
        x_refs = refs[:count]
        w_ref, o_ref, all_x, acc = refs[count:]
        part = pl.program_id(0)

        @pl.when(part == 0)
        def _():
            for i in range(count):
                for n in range(STEPS):
                    all_x[n, i * rows : (i + 1) * rows, :] = x_refs[i][:, n * step : (n + 1) * step]
            acc[...] = jnp.zeros_like(acc)

        for j in range(kinds):
            lanes = slice(j * third, (j + 1) * third)
            acc[:, lanes] += jnp.dot(all_x[part], w_ref[j], preferred_element_type=jnp.float32)

        @pl.when(part == STEPS - 1)
        def _():
            nt = (((1,), (1,)), ((), ()))
            lead = (lax.broadcasted_iota(jnp.int32, (8, EDGE), 1) == 0).astype(jnp.bfloat16)
            edge = jnp.concatenate([x_refs[i][:, width:] for i in range(count)], axis=0)
            code = lax.dot_general(lead, edge, nt, preferred_element_type=jnp.float32)[:1].astype(jnp.int32)
            row = lax.broadcasted_iota(jnp.int32, (1, count * rows), 1)
            slot = (code // CAP) * each + (row // rows) * CAP + code % CAP
            pick = (lax.broadcasted_iota(jnp.int32, (slots, count * rows), 0) == slot).astype(jnp.bfloat16)
            ones = jnp.ones((count * rows, EDGE), jnp.bfloat16)
            filled = jnp.dot(pick, ones, preferred_element_type=jnp.float32)[:, :1] > 0
            for j in range(kinds):
                lanes = slice(j * third, (j + 1) * third)
                placed = jnp.dot(pick, acc[:, lanes].astype(jnp.bfloat16), preferred_element_type=jnp.float32)
                placed = jnp.where(filled, placed, EMPTY).astype(jnp.bfloat16)
                o_ref[:, :, lanes] = placed.reshape(owners, each, third)

    full = pl.BlockSpec((rows, width + EDGE), lambda part: (0, 0))
    return pl.pallas_call(
        body,
        grid=(STEPS,),
        in_specs=[full] * count + [pl.BlockSpec((kinds, step, third), lambda part: (0, part, 0))],
        out_specs=pl.BlockSpec((owners, each, cols), lambda part: (0, 0, 0)),
        out_shape=jax.ShapeDtypeStruct((owners, each, cols), jnp.bfloat16),
        scratch_shapes=[
            pltpu.VMEM((STEPS, count * rows, step), jnp.bfloat16),
            pltpu.VMEM((count * rows, cols), jnp.float32),
        ],
        compiler_params=pltpu.CompilerParams(vmem_limit_bytes=40 << 20),
        cost_estimate=pl.CostEstimate(
            flops=2 * count * rows * width * cols,
            transcendentals=0,
            bytes_accessed=2 * width * cols + 2 * count * rows * width,
        ),
        name="project",
    )(*blocks, pltpu.with_memory_space_constraint(weight, pltpu.HBM))


def by_source(part, cols):
    owners, each, _ = part.shape
    chunk, span = owners * each, owners * CAP
    new = lax.broadcasted_iota(jnp.int32, (chunk, chunk), 0)
    old = lax.broadcasted_iota(jnp.int32, (chunk, chunk), 1)
    source, rest = new // span, new % span
    move = ((rest // CAP) * each + source * CAP + rest % CAP == old).astype(jnp.bfloat16)
    return jnp.dot(move, part.reshape(chunk, cols), preferred_element_type=jnp.float32).astype(jnp.bfloat16)


def assemble(parts):
    owners, each, cols = parts[0].shape
    chunk = owners * each

    def body(*refs):
        for c in range(len(parts)):
            refs[-1][c * chunk : (c + 1) * chunk, :] = by_source(refs[c][...], cols)

    vmem = pl.BlockSpec(memory_space=pltpu.VMEM)
    return pl.pallas_call(
        body,
        in_specs=[vmem] * len(parts),
        out_specs=vmem,
        out_shape=jax.ShapeDtypeStruct((len(parts) * chunk, cols), jnp.bfloat16),
        compiler_params=pltpu.CompilerParams(vmem_limit_bytes=16 << 20),
        cost_estimate=pl.CostEstimate(
            flops=2 * len(parts) * chunk * chunk * cols, transcendentals=0, bytes_accessed=4 * len(parts) * chunk * cols
        ),
        name="assemble",
    )(*parts)


def attention(early, last, where_to, segments, cotangent):
    owners, each, cols = last.shape
    pack_len = cotangent.shape[0]
    third = cols // 3
    heads = third // HD
    span = owners * CAP
    block = 256
    blocks = pack_len // block
    scale = HD ** (-0.5)
    nt = (((1,), (1,)), ((), ()))
    tn = (((0,), (0,)), ((), ()))
    f32 = jnp.float32

    def body(*refs):
        early_ref, last_ref = refs[:2]
        to_ref, segk_ref, segq_ref, cot_ref, out_ref, grad_ref, qkv, keep, codes, dk, dv, low = refs[2:]
        before = early.shape[0] // span
        late = by_source(last_ref[...], cols)
        for i in range(before + each // CAP):
            at = pl.multiple_of(to_ref[i] * span, span)
            if i < before:
                qkv[pl.ds(at, span), :] = early_ref[i * span : (i + 1) * span, :]
            else:
                qkv[pl.ds(at, span), :] = late[(i - before) * span : (i - before + 1) * span, :]
        for b in range(blocks):
            at = b * block
            lead = qkv[at : at + block, :HD].astype(f32)
            live = (lead < 0.5 * EMPTY).astype(f32)
            keep[at : at + block, :] = live
            held = qkv[at : at + block, :]
            qkv[at : at + block, :] = jnp.where(live[:, :1] > 0, held, jnp.zeros_like(held))
            live_row = (lead.T[:1, :] < 0.5 * EMPTY)
            seg = segk_ref[:, at : at + block]
            codes[:, at : at + block] = jnp.where(live_row, seg, -1)

        def clear():
            dk[...] = jnp.zeros_like(dk)
            dv[...] = jnp.zeros_like(dv)
            low[...] = jnp.zeros_like(low)

        def work(at, start, size):
            rows = pl.ds(at, block)
            win = pl.ds(start, size)
            live = keep[rows, :]
            allowed = segq_ref[rows, :] == codes[:, win]
            for h in range(heads):
                lanes = slice(h * HD, (h + 1) * HD)
                q = qkv[rows, h * HD : (h + 1) * HD]
                k = qkv[win, third + h * HD : third + (h + 1) * HD]
                v = qkv[win, 2 * third + h * HD : 2 * third + (h + 1) * HD]
                s = lax.dot_general(q, k, nt, preferred_element_type=f32) * scale
                s = jnp.where(allowed, s, FILL)
                top = jnp.max(s, axis=1, keepdims=True)
                e = jnp.exp(s - top)
                p = e * (1.0 / jnp.sum(e, axis=1, keepdims=True))
                p_low = p.astype(jnp.bfloat16)
                context = jnp.dot(p_low, v, preferred_element_type=f32)
                out_ref[rows, lanes] = (context * live).astype(jnp.bfloat16)
                g32 = cot_ref[rows, lanes].astype(f32) * live
                g = g32.astype(jnp.bfloat16)
                delta = jnp.sum(g32 * context, axis=1, keepdims=True)
                dp = lax.dot_general(g, v, nt, preferred_element_type=f32)
                ds = (p * (dp - delta)).astype(jnp.bfloat16)
                dq = jnp.dot(ds, k, preferred_element_type=f32) * scale
                grad_ref[0, rows, lanes] = dq.astype(jnp.bfloat16)
                dk[win, lanes] += lax.dot_general(ds, q, tn, preferred_element_type=f32)
                dv[win, lanes] += lax.dot_general(p_low, g, tn, preferred_element_type=f32)
                low[...] = jnp.minimum(low[...], jnp.min(jnp.where(live > 0, top, 0.0), axis=0, keepdims=True))

        clear()
        for b in range(blocks):
            first, last = max(b - 1, 0), min(b + 2, blocks)
            work(b * block, first * block, (last - first) * block)

        @pl.when(jnp.min(low[...]) < 0.5 * FILL)
        def _():
            clear()

            def again(b, carry):
                work(pl.multiple_of(b * block, block), 0, pack_len)
                return carry

            lax.fori_loop(0, blocks, again, 0)

        grad_ref[1] = (dk[...] * scale).astype(jnp.bfloat16)
        grad_ref[2] = dv[...].astype(jnp.bfloat16)

    vmem = pl.BlockSpec(memory_space=pltpu.VMEM)
    return pl.pallas_call(
        body,
        in_specs=[vmem] * 2 + [pl.BlockSpec(memory_space=pltpu.SMEM)] + [vmem] * 3,
        out_specs=[vmem, vmem],
        out_shape=[
            jax.ShapeDtypeStruct((pack_len, third), jnp.bfloat16),
            jax.ShapeDtypeStruct((3, pack_len, third), jnp.bfloat16),
        ],
        scratch_shapes=[
            pltpu.VMEM((pack_len, cols), jnp.bfloat16),
            pltpu.VMEM((pack_len, HD), f32),
            pltpu.VMEM((1, pack_len), jnp.int32),
            pltpu.VMEM((pack_len, third), f32),
            pltpu.VMEM((pack_len, third), f32),
            pltpu.VMEM((8, HD), f32),
        ],
        compiler_params=pltpu.CompilerParams(vmem_limit_bytes=50 << 20),
        cost_estimate=pl.CostEstimate(
            flops=12 * pack_len * pack_len * third, transcendentals=pack_len * pack_len * heads, bytes_accessed=1 << 23
        ),
        name="attention",
    )(early, last, where_to, segments, segments.reshape(pack_len, 1), cotangent)


def receive(block, link):
    pairs = [
        (((y + link[1]) % SIDE) * SIDE + (x + link[0]) % SIDE, y * SIDE + x)
        for y in range(SIDE)
        for x in range(SIDE)
    ]
    return lax.ppermute(block, "seq", pairs)


def per_device(patches, destination, segments, qkv_weight, cotangent):
    owners = lax.axis_size("dp")
    weight = jnp.transpose(qkv_weight, (1, 0, 2))

    held = {(0, 0): mark_rows(patches, destination)}
    for turn in ROUNDS:
        for (dx, dy), (lx, ly) in turn:
            held[dx, dy] = receive(held[(dx - lx) % SIDE, (dy - ly) % SIDE], (lx, ly))
    order = [offset for turn in ROUNDS for offset, _ in turn] + [(0, 0)]
    arrived = [order[:4], order[4:8], order[8:12], order[12:]]
    parts = []
    for offsets in arrived:
        placed = project([held[offset] for offset in offsets], weight, owners)
        parts.append(lax.all_to_all(placed, "dp", split_axis=0, concat_axis=0, tiled=True))

    here = lax.axis_index("seq")
    hx, hy = here % SIDE, here // SIDE
    where_to = jnp.stack([((hy + dy) % SIDE) * SIDE + (hx + dx) % SIDE for turn in arrived for dx, dy in turn])

    attended, grads = attention(assemble(parts[:-1]), parts[-1], where_to, segments, cotangent[0])
    return attended[None], jnp.transpose(grads, (1, 0, 2))[None]


def solution(mesh):
    in_specs = (
        P(("dp", "seq"), None),
        P(("dp", "seq"), None),
        P("dp", None),
        P(None, None, "seq"),
        P("dp", None, "seq"),
    )
    out_specs = (P("dp", None, "seq"), P("dp", None, None, "seq"))
    return jax.shard_map(per_device, mesh=mesh, in_specs=in_specs, out_specs=out_specs, check_vma=False)
```

```python
import jax
import jax.numpy as jnp
from jax import lax
from jax.experimental import pallas as pl
from jax.experimental.pallas import tpu as pltpu
from jax.sharding import PartitionSpec as P

HD = 128
SIDE = 4
CAP = 4
FILL = -1000000000.0
EMPTY = 1.0e15
EDGE = 128
STEPS = 2

ROUNDS = (
    (((1, 0), (1, 0)), ((3, 0), (3, 0)), ((0, 1), (0, 1)), ((0, 3), (0, 3))),
    (((1, 1), (1, 0)), ((3, 1), (0, 1)), ((3, 3), (3, 0)), ((1, 3), (0, 3))),
    (((2, 1), (1, 0)), ((2, 3), (3, 0)), ((3, 2), (0, 1)), ((1, 2), (0, 3))),
    (((2, 0), (1, 0)), ((0, 2), (0, 1)), ((2, 2), (3, 0))),
)


def mark_rows(patches, destination):
    rows, width = patches.shape

    def body(x_ref, t_ref, o_ref):
        o_ref[:, :width] = x_ref[...]
        owner = lax.broadcasted_iota(jnp.int32, (EDGE, rows), 0)
        onehot = (t_ref[...] == owner).astype(jnp.bfloat16)
        r = lax.broadcasted_iota(jnp.int32, (rows, rows), 0)
        c = lax.broadcasted_iota(jnp.int32, (rows, rows), 1)
        earlier = (r < c).astype(jnp.bfloat16)
        before = jnp.dot(onehot, earlier, preferred_element_type=jnp.float32)
        rank = (before * onehot.astype(jnp.float32)).astype(jnp.bfloat16)
        number = (lax.broadcasted_iota(jnp.int32, (EDGE, EDGE), 0) * CAP).astype(jnp.float32).astype(jnp.bfloat16)
        tn = (((0,), (0,)), ((), ()))
        slot = lax.dot_general(onehot, number, tn, preferred_element_type=jnp.float32)
        slot += lax.dot_general(rank, jnp.ones((EDGE, EDGE), jnp.bfloat16), tn, preferred_element_type=jnp.float32)
        o_ref[:, width:] = slot.astype(jnp.bfloat16)

    return pl.pallas_call(
        body,
        out_shape=jax.ShapeDtypeStruct((rows, width + EDGE), jnp.bfloat16),
        name="mark_rows",
    )(patches, destination.reshape(1, rows))


def project(blocks, weight, owners):
    count = len(blocks)
    rows = blocks[0].shape[0]
    kinds, width, third = weight.shape
    cols = kinds * third
    each = CAP * count
    slots = owners * each
    step = width // STEPS

    def body(*refs):
        x_refs = refs[:count]
        w_ref, o_ref, all_x, acc = refs[count:]
        part = pl.program_id(0)

        @pl.when(part == 0)
        def _():
            for i in range(count):
                for n in range(STEPS):
                    all_x[n, i * rows : (i + 1) * rows, :] = x_refs[i][:, n * step : (n + 1) * step]
            acc[...] = jnp.zeros_like(acc)

        for j in range(kinds):
            lanes = slice(j * third, (j + 1) * third)
            acc[:, lanes] += jnp.dot(all_x[part], w_ref[j], preferred_element_type=jnp.float32)

        @pl.when(part == STEPS - 1)
        def _():
            nt = (((1,), (1,)), ((), ()))
            lead = (lax.broadcasted_iota(jnp.int32, (8, EDGE), 1) == 0).astype(jnp.bfloat16)
            edge = jnp.concatenate([x_refs[i][:, width:] for i in range(count)], axis=0)
            code = lax.dot_general(lead, edge, nt, preferred_element_type=jnp.float32)[:1].astype(jnp.int32)
            row = lax.broadcasted_iota(jnp.int32, (1, count * rows), 1)
            slot = (code // CAP) * each + (row // rows) * CAP + code % CAP
            pick = (lax.broadcasted_iota(jnp.int32, (slots, count * rows), 0) == slot).astype(jnp.bfloat16)
            ones = jnp.ones((count * rows, EDGE), jnp.bfloat16)
            filled = jnp.dot(pick, ones, preferred_element_type=jnp.float32)[:, :1] > 0
            for j in range(kinds):
                lanes = slice(j * third, (j + 1) * third)
                placed = jnp.dot(pick, acc[:, lanes].astype(jnp.bfloat16), preferred_element_type=jnp.float32)
                placed = jnp.where(filled, placed, EMPTY).astype(jnp.bfloat16)
                o_ref[:, :, lanes] = placed.reshape(owners, each, third)

    full = pl.BlockSpec((rows, width + EDGE), lambda part: (0, 0))
    return pl.pallas_call(
        body,
        grid=(STEPS,),
        in_specs=[full] * count + [pl.BlockSpec((kinds, step, third), lambda part: (0, part, 0))],
        out_specs=pl.BlockSpec((owners, each, cols), lambda part: (0, 0, 0)),
        out_shape=jax.ShapeDtypeStruct((owners, each, cols), jnp.bfloat16),
        scratch_shapes=[
            pltpu.VMEM((STEPS, count * rows, step), jnp.bfloat16),
            pltpu.VMEM((count * rows, cols), jnp.float32),
        ],
        compiler_params=pltpu.CompilerParams(vmem_limit_bytes=40 << 20),
        cost_estimate=pl.CostEstimate(
            flops=2 * count * rows * width * cols,
            transcendentals=0,
            bytes_accessed=2 * width * cols + 2 * count * rows * width,
        ),
        name="project",
    )(*blocks, pltpu.with_memory_space_constraint(weight, pltpu.HBM))


def by_source(part, cols):
    owners, each, _ = part.shape
    chunk, span = owners * each, owners * CAP
    new = lax.broadcasted_iota(jnp.int32, (chunk, chunk), 0)
    old = lax.broadcasted_iota(jnp.int32, (chunk, chunk), 1)
    source, rest = new // span, new % span
    move = ((rest // CAP) * each + source * CAP + rest % CAP == old).astype(jnp.bfloat16)
    return jnp.dot(move, part.reshape(chunk, cols), preferred_element_type=jnp.float32).astype(jnp.bfloat16)


def assemble(parts):
    owners, each, cols = parts[0].shape
    chunk = owners * each

    def body(*refs):
        for c in range(len(parts)):
            refs[-1][c * chunk : (c + 1) * chunk, :] = by_source(refs[c][...], cols)

    vmem = pl.BlockSpec(memory_space=pltpu.VMEM)
    return pl.pallas_call(
        body,
        in_specs=[vmem] * len(parts),
        out_specs=vmem,
        out_shape=jax.ShapeDtypeStruct((len(parts) * chunk, cols), jnp.bfloat16),
        compiler_params=pltpu.CompilerParams(vmem_limit_bytes=16 << 20),
        cost_estimate=pl.CostEstimate(
            flops=2 * len(parts) * chunk * chunk * cols, transcendentals=0, bytes_accessed=4 * len(parts) * chunk * cols
        ),
        name="assemble",
    )(*parts)


def attention(early, last, where_to, segments, cotangent):
    owners, each, cols = last.shape
    pack_len = cotangent.shape[0]
    third = cols // 3
    heads = third // HD
    span = owners * CAP
    block = 256
    blocks = pack_len // block
    scale = HD ** (-0.5)
    nt = (((1,), (1,)), ((), ()))
    tn = (((0,), (0,)), ((), ()))
    f32 = jnp.float32

    def body(*refs):
        early_ref, last_ref = refs[:2]
        to_ref, segk_ref, segq_ref, cot_hbm, out_ref, grad_ref, cot_ref, cot_here, qkv, keep, codes, dk, dv, low = refs[2:]
        load = pltpu.make_async_copy(cot_hbm, cot_ref, cot_here)
        load.start()
        before = early.shape[0] // span
        late = by_source(last_ref[...], cols)
        for i in range(before + each // CAP):
            at = pl.multiple_of(to_ref[i] * span, span)
            if i < before:
                qkv[pl.ds(at, span), :] = early_ref[i * span : (i + 1) * span, :]
            else:
                qkv[pl.ds(at, span), :] = late[(i - before) * span : (i - before + 1) * span, :]
        for b in range(blocks):
            at = b * block
            lead = qkv[at : at + block, :HD].astype(f32)
            live = (lead < 0.5 * EMPTY).astype(f32)
            keep[at : at + block, :] = live
            held = qkv[at : at + block, :]
            qkv[at : at + block, :] = jnp.where(live[:, :1] > 0, held, jnp.zeros_like(held))
            live_row = (lead.T[:1, :] < 0.5 * EMPTY)
            seg = segk_ref[:, at : at + block]
            codes[:, at : at + block] = jnp.where(live_row, seg, -1)

        def clear():
            dk[...] = jnp.zeros_like(dk)
            dv[...] = jnp.zeros_like(dv)
            low[...] = jnp.zeros_like(low)

        def work(at, start, size):
            rows = pl.ds(at, block)
            win = pl.ds(start, size)
            live = keep[rows, :]
            allowed = segq_ref[rows, :] == codes[:, win]
            for h in range(heads):
                lanes = slice(h * HD, (h + 1) * HD)
                q = qkv[rows, h * HD : (h + 1) * HD]
                k = qkv[win, third + h * HD : third + (h + 1) * HD]
                v = qkv[win, 2 * third + h * HD : 2 * third + (h + 1) * HD]
                s = lax.dot_general(q, k, nt, preferred_element_type=f32) * scale
                s = jnp.where(allowed, s, FILL)
                top = jnp.max(s, axis=1, keepdims=True)
                e = jnp.exp(s - top)
                p = e * (1.0 / jnp.sum(e, axis=1, keepdims=True))
                p_low = p.astype(jnp.bfloat16)
                context = jnp.dot(p_low, v, preferred_element_type=f32)
                out_ref[rows, lanes] = (context * live).astype(jnp.bfloat16)
                g32 = cot_ref[rows, lanes].astype(f32) * live
                g = g32.astype(jnp.bfloat16)
                delta = jnp.sum(g32 * context, axis=1, keepdims=True)
                dp = lax.dot_general(g, v, nt, preferred_element_type=f32)
                ds = (p * (dp - delta)).astype(jnp.bfloat16)
                dq = jnp.dot(ds, k, preferred_element_type=f32) * scale
                grad_ref[0, rows, lanes] = dq.astype(jnp.bfloat16)
                dk[win, lanes] += lax.dot_general(ds, q, tn, preferred_element_type=f32)
                dv[win, lanes] += lax.dot_general(p_low, g, tn, preferred_element_type=f32)
                low[...] = jnp.minimum(low[...], jnp.min(jnp.where(live > 0, top, 0.0), axis=0, keepdims=True))

        clear()
        load.wait()
        for b in range(blocks):
            first, last = max(b - 1, 0), min(b + 2, blocks)
            work(b * block, first * block, (last - first) * block)

        @pl.when(jnp.min(low[...]) < 0.5 * FILL)
        def _():
            clear()

            def again(b, carry):
                work(pl.multiple_of(b * block, block), 0, pack_len)
                return carry

            lax.fori_loop(0, blocks, again, 0)

        grad_ref[1] = (dk[...] * scale).astype(jnp.bfloat16)
        grad_ref[2] = dv[...].astype(jnp.bfloat16)

    vmem = pl.BlockSpec(memory_space=pltpu.VMEM)
    return pl.pallas_call(
        body,
        in_specs=[vmem] * 2 + [pl.BlockSpec(memory_space=pltpu.SMEM)] + [vmem] * 2 + [pl.BlockSpec(memory_space=pltpu.HBM)],
        out_specs=[vmem, vmem],
        out_shape=[
            jax.ShapeDtypeStruct((pack_len, third), jnp.bfloat16),
            jax.ShapeDtypeStruct((3, pack_len, third), jnp.bfloat16),
        ],
        scratch_shapes=[
            pltpu.VMEM(cotangent.shape, jnp.bfloat16),
            pltpu.SemaphoreType.DMA,
            pltpu.VMEM((pack_len, cols), jnp.bfloat16),
            pltpu.VMEM((pack_len, HD), f32),
            pltpu.VMEM((1, pack_len), jnp.int32),
            pltpu.VMEM((pack_len, third), f32),
            pltpu.VMEM((pack_len, third), f32),
            pltpu.VMEM((8, HD), f32),
        ],
        compiler_params=pltpu.CompilerParams(vmem_limit_bytes=50 << 20),
        cost_estimate=pl.CostEstimate(
            flops=12 * pack_len * pack_len * third, transcendentals=pack_len * pack_len * heads, bytes_accessed=1 << 23
        ),
        name="attention",
    )(early, last, where_to, segments, segments.reshape(pack_len, 1), pltpu.with_memory_space_constraint(cotangent, pltpu.HBM))


def receive(block, link):
    pairs = [
        (((y + link[1]) % SIDE) * SIDE + (x + link[0]) % SIDE, y * SIDE + x)
        for y in range(SIDE)
        for x in range(SIDE)
    ]
    return lax.ppermute(block, "seq", pairs)


def per_device(patches, destination, segments, qkv_weight, cotangent):
    owners = lax.axis_size("dp")
    weight = jnp.transpose(qkv_weight, (1, 0, 2))

    held = {(0, 0): mark_rows(patches, destination)}
    for turn in ROUNDS:
        for (dx, dy), (lx, ly) in turn:
            held[dx, dy] = receive(held[(dx - lx) % SIDE, (dy - ly) % SIDE], (lx, ly))
    order = [offset for turn in ROUNDS for offset, _ in turn] + [(0, 0)]
    arrived = [order[:4], order[4:8], order[8:12], order[12:]]
    parts = []
    for offsets in arrived:
        placed = project([held[offset] for offset in offsets], weight, owners)
        parts.append(lax.all_to_all(placed, "dp", split_axis=0, concat_axis=0, tiled=True))

    here = lax.axis_index("seq")
    hx, hy = here % SIDE, here // SIDE
    where_to = jnp.stack([((hy + dy) % SIDE) * SIDE + (hx + dx) % SIDE for turn in arrived for dx, dy in turn])

    attended, grads = attention(assemble(parts[:-1]), parts[-1], where_to, segments, cotangent[0])
    return attended[None], jnp.transpose(grads, (1, 0, 2))[None]


def solution(mesh):
    in_specs = (
        P(("dp", "seq"), None),
        P(("dp", "seq"), None),
        P("dp", None),
        P(None, None, "seq"),
        P("dp", None, "seq"),
    )
    out_specs = (P("dp", None, "seq"), P("dp", None, None, "seq"))
    return jax.shard_map(per_device, mesh=mesh, in_specs=in_specs, out_specs=out_specs, check_vma=False)
```

```python
import jax
import jax.numpy as jnp
from jax import lax
from jax.experimental import pallas as pl
from jax.experimental.pallas import tpu as pltpu
from jax.sharding import PartitionSpec as P

HD = 128
SIDE = 4
CAP = 4
FILL = -1000000000.0
LOG2E = 1.4426950408889634
EMPTY = 1.0e15
EDGE = 128
STEPS = 2

ROUNDS = (
    (((1, 0), (1, 0)), ((3, 0), (3, 0)), ((0, 1), (0, 1)), ((0, 3), (0, 3))),
    (((1, 1), (1, 0)), ((3, 1), (0, 1)), ((3, 3), (3, 0)), ((1, 3), (0, 3))),
    (((2, 1), (1, 0)), ((2, 3), (3, 0)), ((3, 2), (0, 1)), ((1, 2), (0, 3))),
    (((2, 0), (1, 0)), ((0, 2), (0, 1)), ((2, 2), (3, 0))),
)


def mark_rows(patches, destination):
    rows, width = patches.shape

    def body(x_ref, t_ref, o_ref):
        o_ref[:, :width] = x_ref[...]
        owner = lax.broadcasted_iota(jnp.int32, (EDGE, rows), 0)
        onehot = (t_ref[...] == owner).astype(jnp.bfloat16)
        r = lax.broadcasted_iota(jnp.int32, (rows, rows), 0)
        c = lax.broadcasted_iota(jnp.int32, (rows, rows), 1)
        earlier = (r < c).astype(jnp.bfloat16)
        before = jnp.dot(onehot, earlier, preferred_element_type=jnp.float32)
        rank = (before * onehot.astype(jnp.float32)).astype(jnp.bfloat16)
        number = (lax.broadcasted_iota(jnp.int32, (EDGE, EDGE), 0) * CAP).astype(jnp.float32).astype(jnp.bfloat16)
        tn = (((0,), (0,)), ((), ()))
        slot = lax.dot_general(onehot, number, tn, preferred_element_type=jnp.float32)
        slot += lax.dot_general(rank, jnp.ones((EDGE, EDGE), jnp.bfloat16), tn, preferred_element_type=jnp.float32)
        o_ref[:, width:] = slot.astype(jnp.bfloat16)

    return pl.pallas_call(
        body,
        out_shape=jax.ShapeDtypeStruct((rows, width + EDGE), jnp.bfloat16),
        name="mark_rows",
    )(patches, destination.reshape(1, rows))


def project(blocks, weight, owners):
    count = len(blocks)
    rows = blocks[0].shape[0]
    kinds, width, third = weight.shape
    cols = kinds * third
    each = CAP * count
    slots = owners * each
    step = width // STEPS

    def body(*refs):
        x_refs = refs[:count]
        w_ref, o_ref, all_x, acc = refs[count:]
        part = pl.program_id(0)

        @pl.when(part == 0)
        def _():
            for i in range(count):
                for n in range(STEPS):
                    all_x[n, i * rows : (i + 1) * rows, :] = x_refs[i][:, n * step : (n + 1) * step]
            acc[...] = jnp.zeros_like(acc)

        for j in range(kinds):
            lanes = slice(j * third, (j + 1) * third)
            acc[:, lanes] += jnp.dot(all_x[part], w_ref[j], preferred_element_type=jnp.float32)

        @pl.when(part == STEPS - 1)
        def _():
            nt = (((1,), (1,)), ((), ()))
            lead = (lax.broadcasted_iota(jnp.int32, (8, EDGE), 1) == 0).astype(jnp.bfloat16)
            edge = jnp.concatenate([x_refs[i][:, width:] for i in range(count)], axis=0)
            code = lax.dot_general(lead, edge, nt, preferred_element_type=jnp.float32)[:1].astype(jnp.int32)
            row = lax.broadcasted_iota(jnp.int32, (1, count * rows), 1)
            slot = (code // CAP) * each + (row // rows) * CAP + code % CAP
            pick = (lax.broadcasted_iota(jnp.int32, (slots, count * rows), 0) == slot).astype(jnp.bfloat16)
            ones = jnp.ones((count * rows, EDGE), jnp.bfloat16)
            filled = jnp.dot(pick, ones, preferred_element_type=jnp.float32)[:, :1] > 0
            for j in range(kinds):
                lanes = slice(j * third, (j + 1) * third)
                placed = jnp.dot(pick, acc[:, lanes].astype(jnp.bfloat16), preferred_element_type=jnp.float32)
                placed = jnp.where(filled, placed, EMPTY).astype(jnp.bfloat16)
                o_ref[:, :, lanes] = placed.reshape(owners, each, third)

    full = pl.BlockSpec((rows, width + EDGE), lambda part: (0, 0))
    return pl.pallas_call(
        body,
        grid=(STEPS,),
        in_specs=[full] * count + [pl.BlockSpec((kinds, step, third), lambda part: (0, part, 0))],
        out_specs=pl.BlockSpec((owners, each, cols), lambda part: (0, 0, 0)),
        out_shape=jax.ShapeDtypeStruct((owners, each, cols), jnp.bfloat16),
        scratch_shapes=[
            pltpu.VMEM((STEPS, count * rows, step), jnp.bfloat16),
            pltpu.VMEM((count * rows, cols), jnp.float32),
        ],
        compiler_params=pltpu.CompilerParams(vmem_limit_bytes=40 << 20),
        cost_estimate=pl.CostEstimate(
            flops=2 * count * rows * width * cols,
            transcendentals=0,
            bytes_accessed=2 * width * cols + 2 * count * rows * width,
        ),
        name="project",
    )(*blocks, pltpu.with_memory_space_constraint(weight, pltpu.HBM))


def by_source(part, cols):
    owners, each, _ = part.shape
    chunk, span = owners * each, owners * CAP
    new = lax.broadcasted_iota(jnp.int32, (chunk, chunk), 0)
    old = lax.broadcasted_iota(jnp.int32, (chunk, chunk), 1)
    source, rest = new // span, new % span
    move = ((rest // CAP) * each + source * CAP + rest % CAP == old).astype(jnp.bfloat16)
    return jnp.dot(move, part.reshape(chunk, cols), preferred_element_type=jnp.float32).astype(jnp.bfloat16)


def assemble(parts):
    owners, each, cols = parts[0].shape
    chunk = owners * each

    def body(*refs):
        for c in range(len(parts)):
            refs[-1][c * chunk : (c + 1) * chunk, :] = by_source(refs[c][...], cols)

    vmem = pl.BlockSpec(memory_space=pltpu.VMEM)
    return pl.pallas_call(
        body,
        in_specs=[vmem] * len(parts),
        out_specs=vmem,
        out_shape=jax.ShapeDtypeStruct((len(parts) * chunk, cols), jnp.bfloat16),
        compiler_params=pltpu.CompilerParams(vmem_limit_bytes=16 << 20),
        cost_estimate=pl.CostEstimate(
            flops=2 * len(parts) * chunk * chunk * cols, transcendentals=0, bytes_accessed=4 * len(parts) * chunk * cols
        ),
        name="assemble",
    )(*parts)


def attention(early, last, where_to, segments, cotangent):
    owners, each, cols = last.shape
    pack_len = cotangent.shape[0]
    third = cols // 3
    heads = third // HD
    span = owners * CAP
    block = 256
    blocks = pack_len // block
    scale = HD ** (-0.5)
    nt = (((1,), (1,)), ((), ()))
    tn = (((0,), (0,)), ((), ()))
    f32 = jnp.float32

    def body(*refs):
        early_ref, last_ref = refs[:2]
        to_ref, segk_ref, segq_ref, cot_hbm, out_ref, grad_ref, cot_ref, cot_here, qkv, keep, codes, dk, dv, low = refs[2:]
        load = pltpu.make_async_copy(cot_hbm, cot_ref, cot_here)
        load.start()
        before = early.shape[0] // span
        late = by_source(last_ref[...], cols)
        for i in range(before + each // CAP):
            at = pl.multiple_of(to_ref[i] * span, span)
            if i < before:
                qkv[pl.ds(at, span), :] = early_ref[i * span : (i + 1) * span, :]
            else:
                qkv[pl.ds(at, span), :] = late[(i - before) * span : (i - before + 1) * span, :]
        for b in range(blocks):
            at = b * block
            lead = qkv[at : at + block, :HD].astype(f32)
            live = (lead < 0.5 * EMPTY).astype(f32)
            keep[at : at + block, :] = live
            held = qkv[at : at + block, :]
            qkv[at : at + block, :] = jnp.where(live[:, :1] > 0, held, jnp.zeros_like(held))
            live_row = (lead.T[:1, :] < 0.5 * EMPTY)
            seg = segk_ref[:, at : at + block]
            codes[:, at : at + block] = jnp.where(live_row, seg, -1)

        def clear():
            dk[...] = jnp.zeros_like(dk)
            dv[...] = jnp.zeros_like(dv)
            low[...] = jnp.zeros_like(low)

        def work(at, start, size):
            rows = pl.ds(at, block)
            win = pl.ds(start, size)
            live = keep[rows, :]
            allowed = segq_ref[rows, :] == codes[:, win]
            for h in range(heads):
                lanes = slice(h * HD, (h + 1) * HD)
                q = qkv[rows, h * HD : (h + 1) * HD]
                k = qkv[win, third + h * HD : third + (h + 1) * HD]
                v = qkv[win, 2 * third + h * HD : 2 * third + (h + 1) * HD]
                s = lax.dot_general(q, k, nt, preferred_element_type=f32) * (scale * LOG2E)
                s = jnp.where(allowed, s, FILL * LOG2E)
                top = jnp.max(s, axis=1, keepdims=True)
                e = jnp.exp2(s - top)
                p = e * (1.0 / jnp.sum(e, axis=1, keepdims=True))
                p_low = p.astype(jnp.bfloat16)
                context = jnp.dot(p_low, v, preferred_element_type=f32)
                out_ref[rows, lanes] = (context * live).astype(jnp.bfloat16)
                g32 = cot_ref[rows, lanes].astype(f32) * live
                g = g32.astype(jnp.bfloat16)
                delta = jnp.sum(g32 * context, axis=1, keepdims=True)
                dp = lax.dot_general(g, v, nt, preferred_element_type=f32)
                ds = (p * (dp - delta)).astype(jnp.bfloat16)
                dq = jnp.dot(ds, k, preferred_element_type=f32) * scale
                grad_ref[0, rows, lanes] = dq.astype(jnp.bfloat16)
                dk[win, lanes] += lax.dot_general(ds, q, tn, preferred_element_type=f32)
                dv[win, lanes] += lax.dot_general(p_low, g, tn, preferred_element_type=f32)
                low[...] = jnp.minimum(low[...], jnp.min(jnp.where(live > 0, top, 0.0), axis=0, keepdims=True))

        clear()
        load.wait()
        for b in range(blocks):
            first, last = max(b - 1, 0), min(b + 2, blocks)
            work(b * block, first * block, (last - first) * block)

        @pl.when(jnp.min(low[...]) < 0.5 * FILL * LOG2E)
        def _():
            clear()

            def again(b, carry):
                work(pl.multiple_of(b * block, block), 0, pack_len)
                return carry

            lax.fori_loop(0, blocks, again, 0)

        grad_ref[1] = (dk[...] * scale).astype(jnp.bfloat16)
        grad_ref[2] = dv[...].astype(jnp.bfloat16)

    vmem = pl.BlockSpec(memory_space=pltpu.VMEM)
    return pl.pallas_call(
        body,
        in_specs=[vmem] * 2 + [pl.BlockSpec(memory_space=pltpu.SMEM)] + [vmem] * 2 + [pl.BlockSpec(memory_space=pltpu.HBM)],
        out_specs=[vmem, vmem],
        out_shape=[
            jax.ShapeDtypeStruct((pack_len, third), jnp.bfloat16),
            jax.ShapeDtypeStruct((3, pack_len, third), jnp.bfloat16),
        ],
        scratch_shapes=[
            pltpu.VMEM(cotangent.shape, jnp.bfloat16),
            pltpu.SemaphoreType.DMA,
            pltpu.VMEM((pack_len, cols), jnp.bfloat16),
            pltpu.VMEM((pack_len, HD), f32),
            pltpu.VMEM((1, pack_len), jnp.int32),
            pltpu.VMEM((pack_len, third), f32),
            pltpu.VMEM((pack_len, third), f32),
            pltpu.VMEM((8, HD), f32),
        ],
        compiler_params=pltpu.CompilerParams(vmem_limit_bytes=50 << 20),
        cost_estimate=pl.CostEstimate(
            flops=12 * pack_len * pack_len * third, transcendentals=pack_len * pack_len * heads, bytes_accessed=1 << 23
        ),
        name="attention",
    )(early, last, where_to, segments, segments.reshape(pack_len, 1), pltpu.with_memory_space_constraint(cotangent, pltpu.HBM))


def receive(block, link):
    pairs = [
        (((y + link[1]) % SIDE) * SIDE + (x + link[0]) % SIDE, y * SIDE + x)
        for y in range(SIDE)
        for x in range(SIDE)
    ]
    return lax.ppermute(block, "seq", pairs)


def per_device(patches, destination, segments, qkv_weight, cotangent):
    owners = lax.axis_size("dp")
    weight = jnp.transpose(qkv_weight, (1, 0, 2))

    held = {(0, 0): mark_rows(patches, destination)}
    for turn in ROUNDS:
        for (dx, dy), (lx, ly) in turn:
            held[dx, dy] = receive(held[(dx - lx) % SIDE, (dy - ly) % SIDE], (lx, ly))
    order = [offset for turn in ROUNDS for offset, _ in turn] + [(0, 0)]
    arrived = [order[:4], order[4:8], order[8:12], order[12:]]
    parts = []
    for offsets in arrived:
        placed = project([held[offset] for offset in offsets], weight, owners)
        parts.append(lax.all_to_all(placed, "dp", split_axis=0, concat_axis=0, tiled=True))

    here = lax.axis_index("seq")
    hx, hy = here % SIDE, here // SIDE
    where_to = jnp.stack([((hy + dy) % SIDE) * SIDE + (hx + dx) % SIDE for turn in arrived for dx, dy in turn])

    attended, grads = attention(assemble(parts[:-1]), parts[-1], where_to, segments, cotangent[0])
    return attended[None], jnp.transpose(grads, (1, 0, 2))[None]


def solution(mesh):
    in_specs = (
        P(("dp", "seq"), None),
        P(("dp", "seq"), None),
        P("dp", None),
        P(None, None, "seq"),
        P("dp", None, "seq"),
    )
    out_specs = (P("dp", None, "seq"), P("dp", None, None, "seq"))
    return jax.shard_map(per_device, mesh=mesh, in_specs=in_specs, out_specs=out_specs, check_vma=False)
```
